32 devices in a mesh: sub: 1, pts: 32 (over z, y, x, core).
Axes of the slice: x: 2, y: 2, z: 4, core: 2. Of those that a mesh axis runs over, the one named last changes fastest.
Arguments:
- cam_jac: float32 [2, 9, 4, 32768], P(None, None, None, ('sub', 'pts')), may hold values from -3 to 3
- point_jac: float32 [2, 3, 4, 32768], P(None, None, None, ('sub', 'pts')), may hold values from -3 to 3
- residuals: float32 [2, 4, 32768], P(None, None, ('sub', 'pts')), may hold values from -6 to 6
- obs_camera: int32 [4, 32768], P(None, ('sub', 'pts')), may hold values from 0 to 4095
- damping: float32 [1], P('sub'), may hold values from 0.01 to 0.1
Outputs:
- camera_step: float32 [9, 4096], P(None, ('sub', 'pts'))
- point_step: float32 [3, 32768], P(None, ('sub', 'pts'))
The draws below stay inside these ranges and needn't reach their ends.
All inputs are finite; a program needn't handle non-finite values.
Results may differ from the reference program's by a relative error of at most 0.00022.
Values sent between devices are 32-bit elements; how exact they have to be, the bound alone decides.
A program may use at most 64 MiB of HBM per device.

```python
import math
import jax
import jax.numpy as jnp

NCAM = 4096
VIEWS = 4
ITERS = 3
POINTS = 32768


def jacobian_pair(key):
    key = jax.random.fold_in(key, 7)
    key_shared, key_jitter, key_others = jax.random.split(key, 3)
    shared = jnp.clip(jax.random.normal(key_shared, (2, 3, VIEWS, POINTS), jnp.float32), -6.0, 6.0)
    jitter = 0.1 * jnp.clip(jax.random.normal(key_jitter, (2, 3, VIEWS, POINTS), jnp.float32), -6.0, 6.0)
    others = jnp.clip(jax.random.normal(key_others, (2, 6, VIEWS, POINTS), jnp.float32), -6.0, 6.0)
    factor = (2.0 * VIEWS * POINTS / NCAM) ** (-0.5)
    point_part = 0.5 * shared
    camera_part = factor * jnp.concatenate([others[:, :3], jitter - shared, others[:, 3:]], axis=1)
    return (camera_part, point_part)


def draw_cam_jac(key, part):
    camera_part, point_part = jacobian_pair(key)
    return camera_part.astype(jnp.float32)


def draw_point_jac(key, part):
    camera_part, point_part = jacobian_pair(key)
    return point_part.astype(jnp.float32)


def draw_obs_camera(key, part):
    key = jax.random.fold_in(key, 11)
    key_centre, key_offset = jax.random.split(key, 2)
    centre = jax.random.randint(key_centre, (1, POINTS), 0, NCAM, jnp.int32)
    offset = jax.random.randint(key_offset, (VIEWS, POINTS), 0, min(64, NCAM), jnp.int32)
    return ((centre + offset) % NCAM).astype(jnp.int32)


def steps_of(key, shape, pieces, smallest, high):
    level, own = 1.0, jax.random.fold_in(key, 6)
    for position, blocks in pieces:
        draws = jnp.exp(jax.random.uniform(jax.random.fold_in(own, position), (blocks,), jnp.float32, smallest / len(pieces), high / len(pieces)))
        level = level * jnp.repeat(draws, shape[position] // blocks).reshape([-1 if axis == position else 1 for axis in range(len(shape))])
    return level


def centred(rng, shape, scale, limit, cuts=(), held_as=jnp.bfloat16):
    entries = jax.random.normal(rng, shape, jnp.float32) * scale
    if len(cuts) > 0:
        entries = steps_of(rng, shape, cuts, -0.22, 0.18) * entries
    return jnp.clip(entries, min=-limit, max=limit).astype(held_as)


def setup_inputs(seed: int = 0, part: int = 0) -> dict:
    key_list = jax.random.split(jax.random.key(seed), 6)
    part_splits = jax.random.split(jax.random.fold_in(key_list[5], part), 6)
    return {
        "cam_jac": draw_cam_jac(jax.random.fold_in(jax.random.fold_in(key_list[5], part), 71), part),
        "point_jac": draw_point_jac(jax.random.fold_in(jax.random.fold_in(key_list[5], part), 71), part),
        "residuals": centred(part_splits[2], (2, VIEWS, POINTS), 1.0, 6.0, ((2, 32),), jnp.float32),
        "obs_camera": draw_obs_camera(jax.random.fold_in(jax.random.fold_in(key_list[5], part), 71), part),
        "damping": jnp.clip(jnp.exp(jax.random.uniform(part_splits[4], (1,), jnp.float32, math.log(0.01), math.log(0.1))), 0.01, 0.1),
    }


def cofactor(matrix, row, col):
    kept_rows = [other for other in range(3) if other != row]
    kept_cols = [other for other in range(3) if other != col]
    sign = 1.0 if (row + col) % 2 == 0 else -1.0
    first = matrix[kept_rows[0], kept_cols[0]] * matrix[kept_rows[1], kept_cols[1]]
    second = matrix[kept_rows[0], kept_cols[1]] * matrix[kept_rows[1], kept_cols[0]]
    return sign * (first - second)


def point_inverse(point_jac, damp_value):
    gram = jnp.sum(point_jac[:, :, None] * point_jac[:, None, :], axis=(0, 3))
    gram = gram + damp_value * jnp.eye(3, dtype=jnp.float32)[:, :, None]
    determinant = gram[0, 0] * cofactor(gram, 0, 0) + gram[0, 1] * cofactor(gram, 0, 1) + gram[0, 2] * cofactor(gram, 0, 2)
    adjugate = jnp.stack([jnp.stack([cofactor(gram, col, row) for col in range(3)]) for row in range(3)])
    return adjugate / determinant[None, None]


def scatter_cameras(values, obs_camera, cameras):
    flat = values.reshape(values.shape[0], -1)
    return jnp.zeros((values.shape[0], cameras), jnp.float32).at[:, obs_camera.reshape(-1)].add(flat)


def predict(camera_field, cam_jac, obs_camera):
    at_obs = camera_field[:, obs_camera]
    return jnp.sum(cam_jac * at_obs[None], axis=1)


def schur_terms(camera_field, cam_jac, point_jac, obs_camera, inverse, cameras):
    predicted = predict(camera_field, cam_jac, obs_camera)
    pulled = jnp.sum(point_jac * predicted[:, None], axis=(0, 2))
    solved = jnp.sum(inverse * pulled[None], axis=1)
    remain = predicted - jnp.sum(point_jac * solved[None, :, None], axis=1)
    return scatter_cameras(jnp.sum(cam_jac * remain[:, None], axis=0), obs_camera, cameras)


def reference(cam_jac, point_jac, residuals, obs_camera, damping):
    damp_value = damping[0]
    inverse = point_inverse(point_jac, damp_value)
    grad_point = jnp.sum(point_jac * residuals[:, None], axis=(0, 2))
    lifted = jnp.sum(inverse * grad_point[None], axis=1)
    remain = residuals - jnp.sum(point_jac * lifted[None, :, None], axis=1)
    right_side = -scatter_cameras(jnp.sum(cam_jac * remain[:, None], axis=0), obs_camera, NCAM)
    precond = damp_value + scatter_cameras(jnp.sum(cam_jac * cam_jac, axis=0), obs_camera, NCAM)
    solution = jnp.zeros_like(right_side)
    residual_vec = right_side
    scaled = residual_vec / precond
    direction = scaled
    norm_now = jnp.sum(residual_vec * scaled)
    for iteration in range(ITERS):
        image = damp_value * direction + schur_terms(direction, cam_jac, point_jac, obs_camera, inverse, NCAM)
        step_size = norm_now / jnp.sum(direction * image)
        solution = solution + step_size * direction
        residual_vec = residual_vec - step_size * image
        if iteration + 1 < ITERS:
            scaled = residual_vec / precond
            norm_next = jnp.sum(residual_vec * scaled)
            direction = scaled + (norm_next / norm_now) * direction
            norm_now = norm_next
    predicted = predict(solution, cam_jac, obs_camera)
    pulled = grad_point + jnp.sum(point_jac * predicted[:, None], axis=(0, 2))
    point_step = -jnp.sum(inverse * pulled[None], axis=1)
    return solution, point_step
```

```python
import functools

import jax
import jax.numpy as jnp
from jax import lax
from jax.experimental import pallas as pl
from jax.experimental.pallas import tpu as pltpu
from jax.sharding import PartitionSpec as P

NCAM = 4096
ITERS = 3
NT = (((1,), (1,)), ((), ()))


def cofactor(matrix, row, col):
    kept_rows = [other for other in range(3) if other != row]
    kept_cols = [other for other in range(3) if other != col]
    first = matrix[kept_rows[0]][kept_cols[0]] * matrix[kept_rows[1]][kept_cols[1]]
    second = matrix[kept_rows[0]][kept_cols[1]] * matrix[kept_rows[1]][kept_cols[0]]
    return first - second if (row + col) % 2 == 0 else second - first


def rows_sum(block):
    return jnp.sum(block, axis=0, keepdims=True)


def total_of(block):
    return jnp.sum(rows_sum(block), axis=1, keepdims=True)


def pieces_of(block):
    upper = block.astype(jnp.bfloat16)
    lower = (block - upper.astype(jnp.float32)).astype(jnp.bfloat16)
    return upper, lower


def kernel(
    n,
    cam_ref,
    point_ref,
    resid_ref,
    ids_ref,
    damp_ref,
    camera_out,
    point_out,
    hot_ref,
    low_ref,
    jac_ref,
    inv_ref,
    pred_ref,
    remain_ref,
    table_ref,
    first_send,
    first_recv,
    part_send,
    part_recv,
    slice_send,
    slice_recv,
    scalar_send,
    scalar_recv,
    send_sems,
    recv_sems,
):
    me = lax.axis_index("pts")
    views, points = ids_ref.shape
    lanes = camera_out.shape[1]
    params = camera_out.shape[0]
    main = params - 1
    wide = 2 * lanes
    low = n // 2
    damp = damp_ref[0]
    barrier = pltpu.get_barrier_semaphore()

    def greet(step, carry):
        peer = lax.rem(me + 1 + step, n)
        pl.semaphore_signal(
            barrier, inc=1, device_id={"pts": peer}, device_id_type=pl.DeviceIdType.MESH
        )
        return carry

    lax.fori_loop(0, n - 1, greet, 0)

    def exchange(phase, source, target):
        def copy_to(peer, slot):
            return pltpu.make_async_remote_copy(
                src_ref=source(peer),
                dst_ref=target.at[slot],
                send_sem=send_sems.at[phase, peer],
                recv_sem=recv_sems.at[phase, slot],
                device_id={"pts": peer},
                device_id_type=pl.DeviceIdType.MESH,
            )

        def begin(step, carry):
            copy_to(lax.rem(me + 1 + step, n), me).start()
            return carry

        def end(step, carry):
            peer = lax.rem(me + 1 + step, n)
            copy = copy_to(peer, peer)
            copy.wait_recv()
            copy.wait_send()
            return carry

        lax.fori_loop(0, n - 1, begin, 0)
        lax.fori_loop(0, n - 1, end, 0)

    def spread(value):
        return jnp.broadcast_to(value, (1, lanes))

    for view in range(views):
        ids = ids_ref[view : view + 1, :]
        cols = pl.ds(view * points, points)
        lane_ids = lax.bitwise_and(ids, wide - 1) if wide & (wide - 1) == 0 else lax.rem(ids, wide)
        row_ids = (ids - lane_ids) // wide
        high = lax.broadcasted_iota(jnp.int32, (wide, points), 0) == lane_ids
        hot_ref[:, cols] = high.astype(jnp.float32).astype(jnp.bfloat16)
        lows = lax.broadcasted_iota(jnp.int32, (low, points), 0) == row_ids
        low_ref[:, cols] = lows.astype(jnp.float32)
    for coord in range(3):
        jac_ref[coord] = jnp.concatenate([point_ref[0, coord], point_ref[1, coord]], axis=0)

    gram = [[None] * 3 for unused in range(3)]
    for row in range(3):
        for col in range(row, 3):
            entry = rows_sum(jac_ref[row] * jac_ref[col])
            if row == col:
                entry = entry + damp
            gram[row][col] = entry
            gram[col][row] = entry
    determinant = (
        gram[0][0] * cofactor(gram, 0, 0)
        + gram[0][1] * cofactor(gram, 0, 1)
        + gram[0][2] * cofactor(gram, 0, 2)
    )
    for row in range(3):
        for col in range(3):
            inv_ref[3 * row + col : 3 * row + col + 1, :] = cofactor(gram, col, row) / determinant

    def solve(pulled):
        return [
            sum(inv_ref[3 * row + col : 3 * row + col + 1, :] * pulled[col] for col in range(3))
            for row in range(3)
        ]

    def pull(rows):
        return [rows_sum(jac_ref[coord] * rows) for coord in range(3)]

    def push(solved):
        return sum(jac_ref[coord] * solved[coord] for coord in range(3))

    def at_views(view):
        cols = pl.ds(view * points, points)
        return hot_ref[:, cols], low_ref[:, cols]

    def weigh(upper_rows, last_row, lows):
        stacked = [upper_rows * lows[row : row + 1, :] for row in range(low)]
        return jnp.concatenate(stacked + [last_row * lows], axis=0)

    def scatter(values_of):
        totals = None
        for view in range(views):
            hot, lows = at_views(view)
            found = []
            for upper_rows, last_row in values_of(view):
                upper, lower = pieces_of(weigh(upper_rows, last_row, lows))
                found.append(
                    lax.dot_general(upper, hot, NT, preferred_element_type=jnp.float32)
                    + lax.dot_general(lower, hot, NT, preferred_element_type=jnp.float32)
                )
            totals = found if totals is None else [a + b for a, b in zip(totals, found)]
        return totals

    def pulled_values(view):
        first = remain_ref[view : view + 1, :]
        second = remain_ref[views + view : views + view + 1, :]
        return (
            cam_ref[view, 0, 0:main, :] * first + cam_ref[view, 1, 0:main, :] * second,
            cam_ref[view, 0, main:params, :] * first + cam_ref[view, 1, main:params, :] * second,
        )

    def squares(view):
        first, second = cam_ref[view, 0], cam_ref[view, 1]
        both = first * first + second * second
        return both[0:main], both[main:params]

    def fill(target, totals, offset, last):
        for slot in range(n):
            row, half = slot // 2, (slot % 2) * lanes
            target[slot, offset : offset + main, :] = totals[
                row * main : (row + 1) * main, half : half + lanes
            ]
            target[slot, last : last + 1, :] = totals[
                low * main + row : low * main + row + 1, half : half + lanes
            ]

    resid = resid_ref[...]
    grad = pull(resid)
    remain_ref[...] = resid - push(solve(grad))
    right_part, diag_part = scatter(lambda view: [pulled_values(view), squares(view)])
    fill(first_send, -right_part, 0, 2 * main)
    fill(first_send, diag_part, main, 2 * main + 1)
    pl.semaphore_wait(barrier, n - 1)
    first_recv[me] = first_send[me]
    exchange(0, lambda peer: first_send.at[peer], first_recv)
    summed = jnp.sum(first_recv[...], axis=0)
    residual_vec = jnp.concatenate([summed[0:main], summed[2 * main : 2 * main + 1]], axis=0)
    precond = damp + jnp.concatenate(
        [summed[main : 2 * main], summed[2 * main + 1 : 2 * main + 2]], axis=0
    )
    phase = 1
    norm_now = None
    direction = None
    step_sum = None
    pulled_sum = grad
    for iteration in range(ITERS):
        scaled = residual_vec / precond
        slice_send[iteration, 0:params, :] = scaled
        slice_send[iteration, params : params + 1, :] = spread(total_of(residual_vec * scaled))
        mine = slice_recv.at[iteration]
        mine[me] = slice_send[iteration]
        exchange(phase, lambda peer: slice_send.at[iteration], mine)
        phase += 1
        norm_next = jnp.sum(mine[:, params, :], axis=0, keepdims=True)
        factor = None if norm_now is None else norm_next / norm_now
        norm_now = norm_next
        direction = scaled if factor is None else scaled + factor * direction
        for slot in range(n):
            row, half = slot // 2, (slot % 2) * lanes
            spots = (
                (slice(row * main, (row + 1) * main), slice(0, main)),
                (slice(low * main + row, low * main + row + 1), slice(main, params)),
            )
            for spot, source in spots:
                update = mine[slot, source, :]
                if factor is not None:
                    update = update + factor * table_ref[spot, half : half + lanes]
                table_ref[spot, half : half + lanes] = update
        lookup_upper, lookup_lower = pieces_of(table_ref[...])
        for view in range(views):
            hot, lows = at_views(view)
            picked = jnp.dot(lookup_upper, hot, preferred_element_type=jnp.float32) + jnp.dot(
                lookup_lower, hot, preferred_element_type=jnp.float32
            )
            upper_rows = sum(
                picked[row * main : (row + 1) * main] * lows[row : row + 1] for row in range(low)
            )
            last_row = rows_sum(picked[low * main :] * lows)
            for part in range(2):
                pred_ref[part * views + view : part * views + view + 1, :] = (
                    rows_sum(cam_ref[view, part, 0:main, :] * upper_rows)
                    + cam_ref[view, part, main:params, :] * last_row
                )
        predicted = pred_ref[...]
        pulled = pull(predicted)
        remain = predicted - push(solve(pulled))
        curve_part = spread(total_of(predicted * remain) + damp * total_of(direction * direction))
        if iteration + 1 < ITERS:
            remain_ref[...] = remain
            (image_part,) = scatter(lambda view: [pulled_values(view)])
            outgoing = part_send.at[iteration]
            incoming = part_recv.at[iteration]
            fill(outgoing, image_part, 0, main)
            for slot in range(n):
                outgoing[slot, params : params + 1, :] = curve_part
            incoming[me] = outgoing[me]
            exchange(phase, lambda peer: outgoing.at[peer], incoming)
            phase += 1
            summed = jnp.sum(incoming[...], axis=0)
            image = damp * direction + summed[0:params]
            curve = summed[params : params + 1]
        else:
            scalar_send[...] = curve_part
            scalar_recv[me] = curve_part
            exchange(phase, lambda peer: scalar_send, scalar_recv)
            curve = jnp.sum(scalar_recv[...], axis=0)
        step_size = norm_now / curve
        moved = step_size * direction
        step_sum = moved if step_sum is None else step_sum + moved
        wide_step = jnp.concatenate([step_size] * (points // lanes), axis=1)
        pulled_sum = [old + wide_step * new for old, new in zip(pulled_sum, pulled)]
        if iteration + 1 < ITERS:
            residual_vec = residual_vec - step_size * image
    camera_out[...] = step_sum
    solved = solve(pulled_sum)
    for coord in range(3):
        point_out[coord : coord + 1, :] = -solved[coord]


def body(n, cam_jac, point_jac, residuals, obs_camera, damping):
    params = cam_jac.shape[1]
    views, points = obs_camera.shape
    lanes = NCAM // n
    wide, low = 2 * lanes, n // 2
    main = params - 1
    phases = 2 * ITERS + 1
    vmem = functools.partial(pl.BlockSpec, memory_space=pltpu.VMEM)
    return pl.pallas_call(
        functools.partial(kernel, n),
        name="schur_solve",
        out_shape=(
            jax.ShapeDtypeStruct((params, lanes), jnp.float32),
            jax.ShapeDtypeStruct((3, points), jnp.float32),
        ),
        in_specs=[vmem(), vmem(), vmem(), vmem(), pl.BlockSpec(memory_space=pltpu.SMEM)],
        out_specs=(vmem(), vmem()),
        scratch_shapes=[
            pltpu.VMEM((wide, views * points), jnp.bfloat16),
            pltpu.VMEM((low, views * points), jnp.float32),
            pltpu.VMEM((3, 2 * views, points), jnp.float32),
            pltpu.VMEM((9, points), jnp.float32),
            pltpu.VMEM((2 * views, points), jnp.float32),
            pltpu.VMEM((2 * views, points), jnp.float32),
            pltpu.VMEM((low * params, wide), jnp.float32),
            pltpu.VMEM((n, 2 * params, lanes), jnp.float32),
            pltpu.VMEM((n, 2 * params, lanes), jnp.float32),
            pltpu.VMEM((ITERS - 1, n, params + 1, lanes), jnp.float32),
            pltpu.VMEM((ITERS - 1, n, params + 1, lanes), jnp.float32),
            pltpu.VMEM((ITERS, params + 1, lanes), jnp.float32),
            pltpu.VMEM((ITERS, n, params + 1, lanes), jnp.float32),
            pltpu.VMEM((1, lanes), jnp.float32),
            pltpu.VMEM((n, 1, lanes), jnp.float32),
            pltpu.SemaphoreType.DMA((phases, n)),
            pltpu.SemaphoreType.DMA((phases, n)),
        ],
        compiler_params=pltpu.CompilerParams(collective_id=0, has_side_effects=True),
    )(
        cam_jac.transpose(2, 0, 1, 3),
        point_jac,
        residuals.reshape(2 * views, points),
        obs_camera,
        damping,
    )


def solution(mesh):
    in_specs = (
        P(None, None, None, ("sub", "pts")),
        P(None, None, None, ("sub", "pts")),
        P(None, None, ("sub", "pts")),
        P(None, ("sub", "pts")),
        P("sub"),
    )
    out_specs = (P(None, ("sub", "pts")), P(None, ("sub", "pts")))
    return jax.shard_map(
        functools.partial(body, mesh.shape["pts"]),
        mesh=mesh,
        in_specs=in_specs,
        out_specs=out_specs,
        check_vma=False,
    )
```

```python
import functools

import jax
import jax.numpy as jnp
from jax import lax
from jax.experimental import pallas as pl
from jax.experimental.pallas import tpu as pltpu
from jax.sharding import PartitionSpec as P

NCAM = 4096
ITERS = 3
NT = (((1,), (1,)), ((), ()))


def cofactor(matrix, row, col):
    kept_rows = [other for other in range(3) if other != row]
    kept_cols = [other for other in range(3) if other != col]
    first = matrix[kept_rows[0]][kept_cols[0]] * matrix[kept_rows[1]][kept_cols[1]]
    second = matrix[kept_rows[0]][kept_cols[1]] * matrix[kept_rows[1]][kept_cols[0]]
    return first - second if (row + col) % 2 == 0 else second - first


def rows_sum(block):
    return jnp.sum(block, axis=0, keepdims=True)


def total_of(block):
    return jnp.sum(rows_sum(block), axis=1, keepdims=True)


def halves_of(block):
    upper = block.astype(jnp.bfloat16).astype(jnp.float32)
    return upper, block - upper


def kernel(
    n,
    cam_given,
    point_ref,
    resid_ref,
    ids_ref,
    damp_ref,
    camera_out,
    point_out,
    cam_ref,
    hot_ref,
    low_ref,
    jac_ref,
    inv_ref,
    pred_ref,
    remain_ref,
    table_ref,
    first_send,
    first_recv,
    part_send,
    part_recv,
    slice_send,
    slice_recv,
    scalar_send,
    scalar_recv,
    send_sems,
    recv_sems,
):
    me = lax.axis_index("pts")
    views, points = ids_ref.shape
    lanes = camera_out.shape[1]
    params = camera_out.shape[0]
    main = params - 1
    wide = 2 * lanes
    low = n // 2
    damp = damp_ref[0]
    barrier = pltpu.get_barrier_semaphore()
    sent = []

    def greet(step, carry):
        peer = lax.rem(me + 1 + step, n)
        pl.semaphore_signal(
            barrier, inc=1, device_id={"pts": peer}, device_id_type=pl.DeviceIdType.MESH
        )
        return carry

    lax.fori_loop(0, n - 1, greet, 0)

    def exchange(phase, source, target):
        def begin(step, carry):
            peer = lax.rem(me + 1 + lax.rem(step + n // 4, n - 1), n)
            pltpu.make_async_remote_copy(
                src_ref=source(peer),
                dst_ref=target.at[me],
                send_sem=send_sems.at[phase],
                recv_sem=recv_sems.at[phase],
                device_id={"pts": peer},
                device_id_type=pl.DeviceIdType.MESH,
            ).start()
            return carry

        lax.fori_loop(0, n - 1, begin, 0)
        others = target.at[pl.ds(0, n - 1)]
        sent.append(pltpu.make_async_copy(others, others, send_sems.at[phase]))
        pltpu.make_async_copy(others, others, recv_sems.at[phase]).wait()

    def spread(value):
        return jnp.broadcast_to(value, (1, lanes))

    for view in range(views):
        ids = ids_ref[view : view + 1, :]
        cols = pl.ds(view * points, points)
        lane_ids = lax.bitwise_and(ids, wide - 1) if wide & (wide - 1) == 0 else lax.rem(ids, wide)
        row_ids = (ids - lane_ids) // wide
        high = lax.broadcasted_iota(jnp.int32, (wide, points), 0) == lane_ids
        hot_ref[:, cols] = high.astype(jnp.float32).astype(jnp.bfloat16)
        lows = lax.broadcasted_iota(jnp.int32, (low, points), 0) == row_ids
        low_ref[:, cols] = lows.astype(jnp.float32).astype(jnp.bfloat16)
    for view in range(views):
        for part in range(2):
            cam_ref[view, part] = cam_given[part, :, view, :]
    for coord in range(3):
        jac_ref[coord] = jnp.concatenate([point_ref[0, coord], point_ref[1, coord]], axis=0)

    gram = [[None] * 3 for unused in range(3)]
    for row in range(3):
        for col in range(row, 3):
            entry = rows_sum(jac_ref[row] * jac_ref[col])
            if row == col:
                entry = entry + damp
            gram[row][col] = entry
            gram[col][row] = entry
    determinant = (
        gram[0][0] * cofactor(gram, 0, 0)
        + gram[0][1] * cofactor(gram, 0, 1)
        + gram[0][2] * cofactor(gram, 0, 2)
    )
    for row in range(3):
        for col in range(3):
            inv_ref[3 * row + col : 3 * row + col + 1, :] = cofactor(gram, col, row) / determinant

    def solve(pulled):
        return [
            sum(inv_ref[3 * row + col : 3 * row + col + 1, :] * pulled[col] for col in range(3))
            for row in range(3)
        ]

    def pull(rows):
        return [rows_sum(jac_ref[coord] * rows) for coord in range(3)]

    def push(solved):
        return sum(jac_ref[coord] * solved[coord] for coord in range(3))

    def at_views(view):
        cols = pl.ds(view * points, points)
        return hot_ref[:, cols], low_ref[:, cols]

    def scatter(values_of):
        totals = None
        for view in range(views):
            hot, lows = at_views(view)
            stacked = []
            for upper_rows, last_row in values_of(view):
                both = jnp.concatenate(halves_of(upper_rows), axis=0).astype(jnp.bfloat16)
                stacked += [both * lows[row : row + 1, :] for row in range(low)]
                stacked += [half.astype(jnp.bfloat16) * lows for half in halves_of(last_row)]
            found = lax.dot_general(
                jnp.concatenate(stacked, axis=0), hot, NT, preferred_element_type=jnp.float32
            )
            totals = found if totals is None else totals + found
        return totals

    def pulled_values(view):
        first = remain_ref[view : view + 1, :]
        second = remain_ref[views + view : views + view + 1, :]
        return (
            cam_ref[view, 0, 0:main, :] * first + cam_ref[view, 1, 0:main, :] * second,
            cam_ref[view, 0, main:params, :] * first + cam_ref[view, 1, main:params, :] * second,
        )

    def squares(view):
        first, second = cam_ref[view, 0], cam_ref[view, 1]
        both = first * first + second * second
        return both[0:main], both[main:params]

    def fill(target, totals, start, offset, last, sign):
        for slot in range(n):
            row, half = slot // 2, (slot % 2) * lanes
            cols = slice(half, half + lanes)
            first = start + 2 * main * row
            upper = totals[first : first + main, cols] + totals[first + main : first + 2 * main, cols]
            first = start + 2 * main * low + row
            lower = totals[first : first + 1, cols] + totals[first + low : first + low + 1, cols]
            target[slot, offset : offset + main, :] = upper if sign > 0 else -upper
            target[slot, last : last + 1, :] = lower if sign > 0 else -lower

    resid = jnp.concatenate([resid_ref[0], resid_ref[1]], axis=0)
    grad = pull(resid)
    remain_ref[...] = resid - push(solve(grad))
    both_parts = scatter(lambda view: [pulled_values(view), squares(view)])
    fill(first_send, both_parts, 0, 0, 2 * main, -1)
    fill(first_send, both_parts, 2 * low * params, main, 2 * main + 1, 1)
    pl.semaphore_wait(barrier, n - 1)
    first_recv[me] = first_send[me]
    exchange(0, lambda peer: first_send.at[peer], first_recv)
    summed = jnp.sum(first_recv[...], axis=0)
    residual_vec = jnp.concatenate([summed[0:main], summed[2 * main : 2 * main + 1]], axis=0)
    precond = damp + jnp.concatenate(
        [summed[main : 2 * main], summed[2 * main + 1 : 2 * main + 2]], axis=0
    )
    phase = 1
    norm_now = None
    direction = None
    step_sum = None
    pulled_sum = grad
    for iteration in range(ITERS):
        scaled = residual_vec / precond
        slice_send[iteration, 0:params, :] = scaled
        slice_send[iteration, params : params + 1, :] = spread(total_of(residual_vec * scaled))
        mine = slice_recv.at[iteration]
        mine[me] = slice_send[iteration]
        exchange(phase, lambda peer: slice_send.at[iteration], mine)
        phase += 1
        norm_next = jnp.sum(mine[:, params, :], axis=0, keepdims=True)
        factor = None if norm_now is None else norm_next / norm_now
        norm_now = norm_next
        direction = scaled if factor is None else scaled + factor * direction
        for slot in range(n):
            row, half = slot // 2, (slot % 2) * lanes
            spots = (
                (slice(row * main, (row + 1) * main), slice(0, main)),
                (slice(low * main + row, low * main + row + 1), slice(main, params)),
            )
            for spot, source in spots:
                update = mine[slot, source, :]
                if factor is not None:
                    update = update + factor * table_ref[spot, half : half + lanes]
                table_ref[spot, half : half + lanes] = update
        upper, lower = halves_of(table_ref[...])
        lookup = jnp.concatenate([upper, lower], axis=0).astype(jnp.bfloat16)
        for view in range(views):
            hot, lows = at_views(view)
            lows = lows.astype(jnp.float32)
            picked = jnp.dot(lookup, hot, preferred_element_type=jnp.float32)
            size = low * params
            upper_rows = sum(
                (picked[row * main : (row + 1) * main] + picked[size + row * main : size + (row + 1) * main])
                * lows[row : row + 1]
                for row in range(low)
            )
            last_row = rows_sum((picked[low * main : size] + picked[size + low * main :]) * lows)
            for part in range(2):
                pred_ref[part * views + view : part * views + view + 1, :] = (
                    rows_sum(cam_ref[view, part, 0:main, :] * upper_rows)
                    + cam_ref[view, part, main:params, :] * last_row
                )
        predicted = pred_ref[...]
        pulled = pull(predicted)
        remain = predicted - push(solve(pulled))
        curve_part = spread(total_of(predicted * remain) + damp * total_of(direction * direction))
        if iteration + 1 < ITERS:
            remain_ref[...] = remain
            image_part = scatter(lambda view: [pulled_values(view)])
            outgoing = part_send.at[iteration]
            incoming = part_recv.at[iteration]
            fill(outgoing, image_part, 0, 0, main, 1)
            for slot in range(n):
                outgoing[slot, params : params + 1, :] = curve_part
            incoming[me] = outgoing[me]
            exchange(phase, lambda peer: outgoing.at[peer], incoming)
            phase += 1
            summed = jnp.sum(incoming[...], axis=0)
            image = damp * direction + summed[0:params]
            curve = summed[params : params + 1]
        else:
            scalar_send[...] = curve_part
            scalar_recv[me] = curve_part
            exchange(phase, lambda peer: scalar_send, scalar_recv)
            curve = jnp.sum(scalar_recv[...], axis=0)
        step_size = norm_now / curve
        moved = step_size * direction
        step_sum = moved if step_sum is None else step_sum + moved
        wide_step = jnp.concatenate([step_size] * (points // lanes), axis=1)
        pulled_sum = [old + wide_step * new for old, new in zip(pulled_sum, pulled)]
        if iteration + 1 < ITERS:
            residual_vec = residual_vec - step_size * image
    camera_out[...] = step_sum
    for copy in sent:
        copy.wait()
    solved = solve(pulled_sum)
    for coord in range(3):
        point_out[coord : coord + 1, :] = -solved[coord]


def body(n, cam_jac, point_jac, residuals, obs_camera, damping):
    params = cam_jac.shape[1]
    views, points = obs_camera.shape
    lanes = NCAM // n
    wide, low = 2 * lanes, n // 2
    main = params - 1
    phases = 2 * ITERS + 1
    vmem = functools.partial(pl.BlockSpec, memory_space=pltpu.VMEM)
    return pl.pallas_call(
        functools.partial(kernel, n),
        name="schur_solve",
        out_shape=(
            jax.ShapeDtypeStruct((params, lanes), jnp.float32),
            jax.ShapeDtypeStruct((3, points), jnp.float32),
        ),
        in_specs=[vmem(), vmem(), vmem(), vmem(), pl.BlockSpec(memory_space=pltpu.SMEM)],
        out_specs=(vmem(), vmem()),
        scratch_shapes=[
            pltpu.VMEM((views, 2, params, points), jnp.float32),
            pltpu.VMEM((wide, views * points), jnp.bfloat16),
            pltpu.VMEM((low, views * points), jnp.bfloat16),
            pltpu.VMEM((3, 2 * views, points), jnp.float32),
            pltpu.VMEM((9, points), jnp.float32),
            pltpu.VMEM((2 * views, points), jnp.float32),
            pltpu.VMEM((2 * views, points), jnp.float32),
            pltpu.VMEM((low * params, wide), jnp.float32),
            pltpu.VMEM((n, 2 * params, lanes), jnp.float32),
            pltpu.VMEM((n, 2 * params, lanes), jnp.float32),
            pltpu.VMEM((ITERS - 1, n, params + 1, lanes), jnp.float32),
            pltpu.VMEM((ITERS - 1, n, params + 1, lanes), jnp.float32),
            pltpu.VMEM((ITERS, params + 1, lanes), jnp.float32),
            pltpu.VMEM((ITERS, n, params + 1, lanes), jnp.float32),
            pltpu.VMEM((1, lanes), jnp.float32),
            pltpu.VMEM((n, 1, lanes), jnp.float32),
            pltpu.SemaphoreType.DMA((phases,)),
            pltpu.SemaphoreType.DMA((phases,)),
        ],
        compiler_params=pltpu.CompilerParams(collective_id=0, has_side_effects=True),
    )(
        cam_jac,
        point_jac,
        residuals,
        obs_camera,
        damping,
    )


def solution(mesh):
    in_specs = (
        P(None, None, None, ("sub", "pts")),
        P(None, None, None, ("sub", "pts")),
        P(None, None, ("sub", "pts")),
        P(None, ("sub", "pts")),
        P("sub"),
    )
    out_specs = (P(None, ("sub", "pts")), P(None, ("sub", "pts")))
    return jax.shard_map(
        functools.partial(body, mesh.shape["pts"]),
        mesh=mesh,
        in_specs=in_specs,
        out_specs=out_specs,
        check_vma=False,
    )
```

```python
import functools

import jax
import jax.numpy as jnp
from jax import lax
from jax.experimental import pallas as pl
from jax.experimental.pallas import tpu as pltpu
from jax.sharding import PartitionSpec as P

NCAM = 4096
ITERS = 3
GROUP = 4
NT = (((1,), (1,)), ((), ()))


def cofactor(matrix, row, col):
    kept_rows = [other for other in range(3) if other != row]
    kept_cols = [other for other in range(3) if other != col]
    first = matrix[kept_rows[0]][kept_cols[0]] * matrix[kept_rows[1]][kept_cols[1]]
    second = matrix[kept_rows[0]][kept_cols[1]] * matrix[kept_rows[1]][kept_cols[0]]
    return first - second if (row + col) % 2 == 0 else second - first


def rows_sum(block):
    return jnp.sum(block, axis=0, keepdims=True)


def total_of(block):
    return jnp.sum(rows_sum(block), axis=1, keepdims=True)


def halves_of(block):
    upper = block.astype(jnp.bfloat16).astype(jnp.float32)
    return upper, block - upper


def kernel(
    n,
    cam_far,
    point_far,
    resid_far,
    ids_far,
    damp_ref,
    camera_out,
    point_out,
    cam_ref,
    hot_ref,
    low_ref,
    jac_ref,
    inv_ref,
    pred_ref,
    remain_ref,
    table_ref,
    first_send,
    first_recv,
    part_send,
    part_recv,
    slice_send,
    slice_recv,
    scalar_send,
    scalar_recv,
    cam_given,
    point_ref,
    resid_ref,
    ids_ref,
    load_sems,
    send_sems,
    recv_sems,
):
    me = lax.axis_index("pts")
    views, points = ids_ref.shape
    lanes = camera_out.shape[1]
    params = camera_out.shape[0]
    main = params - 1
    wide = GROUP * lanes
    low = n // GROUP
    damp = damp_ref[0]
    barrier = pltpu.get_barrier_semaphore()
    sent = []

    def greet(step, carry):
        peer = lax.rem(me + 1 + step, n)
        pl.semaphore_signal(
            barrier, inc=1, device_id={"pts": peer}, device_id_type=pl.DeviceIdType.MESH
        )
        return carry

    lax.fori_loop(0, n - 1, greet, 0)
    far = (ids_far, cam_far, point_far, resid_far)
    near = (ids_ref, cam_given, point_ref, resid_ref)
    loads = [
        pltpu.make_async_copy(source, target, load_sems.at[spot])
        for spot, (source, target) in enumerate(zip(far, near))
    ]
    for load in loads:
        load.start()
    loads[0].wait()

    def exchange(phase, source, target):
        def begin(step, carry):
            peer = lax.rem(me + 1 + step, n)
            pltpu.make_async_remote_copy(
                src_ref=source(peer),
                dst_ref=target.at[me],
                send_sem=send_sems.at[phase],
                recv_sem=recv_sems.at[phase],
                device_id={"pts": peer},
                device_id_type=pl.DeviceIdType.MESH,
            ).start()
            return carry

        lax.fori_loop(0, n - 1, begin, 0)
        others = target.at[pl.ds(0, n - 1)]
        sent.append(pltpu.make_async_copy(others, others, send_sems.at[phase]))
        pltpu.make_async_copy(others, others, recv_sems.at[phase]).wait()

    def spread(value):
        return jnp.broadcast_to(value, (1, lanes))

    for view in range(views):
        ids = ids_ref[view : view + 1, :]
        cols = pl.ds(view * points, points)
        lane_ids = lax.bitwise_and(ids, wide - 1) if wide & (wide - 1) == 0 else lax.rem(ids, wide)
        row_ids = (ids - lane_ids) // wide
        high = lax.broadcasted_iota(jnp.int32, (wide, points), 0) == lane_ids
        hot_ref[:, cols] = high.astype(jnp.float32).astype(jnp.bfloat16)
        lows = lax.broadcasted_iota(jnp.int32, (low, points), 0) == row_ids
        low_ref[:, cols] = lows.astype(jnp.float32).astype(jnp.bfloat16)
    for load in loads[1:]:
        load.wait()
    for view in range(views):
        for part in range(2):
            cam_ref[view, part] = cam_given[part, :, view, :]
    for coord in range(3):
        jac_ref[coord] = jnp.concatenate([point_ref[0, coord], point_ref[1, coord]], axis=0)

    gram = [[None] * 3 for unused in range(3)]
    for row in range(3):
        for col in range(row, 3):
            entry = rows_sum(jac_ref[row] * jac_ref[col])
            if row == col:
                entry = entry + damp
            gram[row][col] = entry
            gram[col][row] = entry
    determinant = (
        gram[0][0] * cofactor(gram, 0, 0)
        + gram[0][1] * cofactor(gram, 0, 1)
        + gram[0][2] * cofactor(gram, 0, 2)
    )
    for row in range(3):
        for col in range(3):
            inv_ref[3 * row + col : 3 * row + col + 1, :] = cofactor(gram, col, row) / determinant

    def solve(pulled):
        return [
            sum(inv_ref[3 * row + col : 3 * row + col + 1, :] * pulled[col] for col in range(3))
            for row in range(3)
        ]

    def pull(rows):
        return [rows_sum(jac_ref[coord] * rows) for coord in range(3)]

    def push(solved):
        return sum(jac_ref[coord] * solved[coord] for coord in range(3))

    def at_views(view):
        cols = pl.ds(view * points, points)
        return hot_ref[:, cols], low_ref[:, cols]

    def scatter(values_of):
        totals = None
        for view in range(views):
            hot, lows = at_views(view)
            stacked = []
            for upper_rows, last_row in values_of(view):
                both = jnp.concatenate(halves_of(upper_rows), axis=0).astype(jnp.bfloat16)
                stacked += [both * lows[row : row + 1, :] for row in range(low)]
                stacked += [half.astype(jnp.bfloat16) * lows for half in halves_of(last_row)]
            found = lax.dot_general(
                jnp.concatenate(stacked, axis=0), hot, NT, preferred_element_type=jnp.float32
            )
            totals = found if totals is None else totals + found
        return totals

    def pulled_values(view):
        first = remain_ref[view : view + 1, :]
        second = remain_ref[views + view : views + view + 1, :]
        return (
            cam_ref[view, 0, 0:main, :] * first + cam_ref[view, 1, 0:main, :] * second,
            cam_ref[view, 0, main:params, :] * first + cam_ref[view, 1, main:params, :] * second,
        )

    def squares(view):
        first, second = cam_ref[view, 0], cam_ref[view, 1]
        both = first * first + second * second
        return both[0:main], both[main:params]

    def fill(target, totals, start, offset, last, sign):
        for slot in range(n):
            row, half = slot // GROUP, (slot % GROUP) * lanes
            cols = slice(half, half + lanes)
            first = start + 2 * main * row
            upper = totals[first : first + main, cols] + totals[first + main : first + 2 * main, cols]
            first = start + 2 * main * low + row
            lower = totals[first : first + 1, cols] + totals[first + low : first + low + 1, cols]
            target[slot, offset : offset + main, :] = upper if sign > 0 else -upper
            target[slot, last : last + 1, :] = lower if sign > 0 else -lower

    resid = jnp.concatenate([resid_ref[0], resid_ref[1]], axis=0)
    grad = pull(resid)
    remain_ref[...] = resid - push(solve(grad))
    both_parts = scatter(lambda view: [pulled_values(view), squares(view)])
    fill(first_send, both_parts, 0, 0, 2 * main, -1)
    fill(first_send, both_parts, 2 * low * params, main, 2 * main + 1, 1)
    pl.semaphore_wait(barrier, n - 1)
    first_recv[me] = first_send[me]
    exchange(0, lambda peer: first_send.at[peer], first_recv)
    summed = jnp.sum(first_recv[...], axis=0)
    residual_vec = jnp.concatenate([summed[0:main], summed[2 * main : 2 * main + 1]], axis=0)
    precond = damp + jnp.concatenate(
        [summed[main : 2 * main], summed[2 * main + 1 : 2 * main + 2]], axis=0
    )
    phase = 1
    norm_now = None
    direction = None
    step_sum = None
    pulled_sum = grad
    for iteration in range(ITERS):
        scaled = residual_vec / precond
        slice_send[iteration, 0:params, :] = scaled
        slice_send[iteration, params : params + 1, :] = spread(total_of(residual_vec * scaled))
        mine = slice_recv.at[iteration]
        mine[me] = slice_send[iteration]
        exchange(phase, lambda peer: slice_send.at[iteration], mine)
        phase += 1
        norm_next = jnp.sum(mine[:, params, :], axis=0, keepdims=True)
        factor = None if norm_now is None else norm_next / norm_now
        norm_now = norm_next
        direction = scaled if factor is None else scaled + factor * direction
        for slot in range(n):
            row, half = slot // GROUP, (slot % GROUP) * lanes
            spots = (
                (slice(row * main, (row + 1) * main), slice(0, main)),
                (slice(low * main + row, low * main + row + 1), slice(main, params)),
            )
            for spot, source in spots:
                update = mine[slot, source, :]
                if factor is not None:
                    update = update + factor * table_ref[spot, half : half + lanes]
                table_ref[spot, half : half + lanes] = update
        upper, lower = halves_of(table_ref[...])
        lookup = jnp.concatenate([upper, lower], axis=0).astype(jnp.bfloat16)
        for view in range(views):
            hot, lows = at_views(view)
            lows = lows.astype(jnp.float32)
            picked = jnp.dot(lookup, hot, preferred_element_type=jnp.float32)
            size = low * params
            upper_rows = sum(
                (picked[row * main : (row + 1) * main] + picked[size + row * main : size + (row + 1) * main])
                * lows[row : row + 1]
                for row in range(low)
            )
            last_row = rows_sum((picked[low * main : size] + picked[size + low * main :]) * lows)
            for part in range(2):
                pred_ref[part * views + view : part * views + view + 1, :] = (
                    rows_sum(cam_ref[view, part, 0:main, :] * upper_rows)
                    + cam_ref[view, part, main:params, :] * last_row
                )
        predicted = pred_ref[...]
        pulled = pull(predicted)
        remain = predicted - push(solve(pulled))
        curve_part = spread(total_of(predicted * remain) + damp * total_of(direction * direction))
        if iteration + 1 < ITERS:
            remain_ref[...] = remain
            image_part = scatter(lambda view: [pulled_values(view)])
            outgoing = part_send.at[iteration]
            incoming = part_recv.at[iteration]
            fill(outgoing, image_part, 0, 0, main, 1)
            for slot in range(n):
                outgoing[slot, params : params + 1, :] = curve_part
            incoming[me] = outgoing[me]
            exchange(phase, lambda peer: outgoing.at[peer], incoming)
            phase += 1
            summed = jnp.sum(incoming[...], axis=0)
            image = damp * direction + summed[0:params]
            curve = summed[params : params + 1]
        else:
            scalar_send[...] = curve_part
            scalar_recv[me] = curve_part
            exchange(phase, lambda peer: scalar_send, scalar_recv)
            curve = jnp.sum(scalar_recv[...], axis=0)
        step_size = norm_now / curve
        moved = step_size * direction
        step_sum = moved if step_sum is None else step_sum + moved
        wide_step = jnp.concatenate([step_size] * (points // lanes), axis=1)
        pulled_sum = [old + wide_step * new for old, new in zip(pulled_sum, pulled)]
        if iteration + 1 < ITERS:
            residual_vec = residual_vec - step_size * image
    camera_out[...] = step_sum
    for copy in sent:
        copy.wait()
    solved = solve(pulled_sum)
    for coord in range(3):
        point_out[coord : coord + 1, :] = solved[coord]


def hand_on(camera_ref, point_ref, camera_out, point_out):
    camera_out[...] = camera_ref[...]
    point_out[...] = -point_ref[...]


def body(n, cam_jac, point_jac, residuals, obs_camera, damping):
    params = cam_jac.shape[1]
    views, points = obs_camera.shape
    lanes = NCAM // n
    wide, low = GROUP * lanes, n // GROUP
    main = params - 1
    phases = 2 * ITERS + 1
    vmem = functools.partial(pl.BlockSpec, memory_space=pltpu.VMEM)
    camera_step, point_step = pl.pallas_call(
        functools.partial(kernel, n),
        name="schur_solve",
        out_shape=(
            jax.ShapeDtypeStruct((params, lanes), jnp.float32),
            jax.ShapeDtypeStruct((3, points), jnp.float32),
        ),
        in_specs=[pl.BlockSpec(memory_space=pl.ANY)] * 4 + [pl.BlockSpec(memory_space=pltpu.SMEM)],
        out_specs=(vmem(), vmem()),
        scratch_shapes=[
            pltpu.VMEM((views, 2, params, points), jnp.float32),
            pltpu.VMEM((wide, views * points), jnp.bfloat16),
            pltpu.VMEM((low, views * points), jnp.bfloat16),
            pltpu.VMEM((3, 2 * views, points), jnp.float32),
            pltpu.VMEM((9, points), jnp.float32),
            pltpu.VMEM((2 * views, points), jnp.float32),
            pltpu.VMEM((2 * views, points), jnp.float32),
            pltpu.VMEM((low * params, wide), jnp.float32),
            pltpu.VMEM((n, 2 * params, lanes), jnp.float32),
            pltpu.VMEM((n, 2 * params, lanes), jnp.float32),
            pltpu.VMEM((ITERS - 1, n, params + 1, lanes), jnp.float32),
            pltpu.VMEM((ITERS - 1, n, params + 1, lanes), jnp.float32),
            pltpu.VMEM((ITERS, params + 1, lanes), jnp.float32),
            pltpu.VMEM((ITERS, n, params + 1, lanes), jnp.float32),
            pltpu.VMEM((1, lanes), jnp.float32),
            pltpu.VMEM((n, 1, lanes), jnp.float32),
            pltpu.VMEM(cam_jac.shape, jnp.float32),
            pltpu.VMEM(point_jac.shape, jnp.float32),
            pltpu.VMEM(residuals.shape, jnp.float32),
            pltpu.VMEM(obs_camera.shape, jnp.int32),
            pltpu.SemaphoreType.DMA((4,)),
            pltpu.SemaphoreType.DMA((phases,)),
            pltpu.SemaphoreType.DMA((phases,)),
        ],
        compiler_params=pltpu.CompilerParams(collective_id=0, has_side_effects=True),
    )(
        cam_jac,
        point_jac,
        residuals,
        obs_camera,
        damping,
    )
    return pl.pallas_call(
        hand_on,
        name="hand_on",
        out_shape=(
            jax.ShapeDtypeStruct(camera_step.shape, jnp.float32),
            jax.ShapeDtypeStruct(point_step.shape, jnp.float32),
        ),
        in_specs=[vmem(), vmem()],
        out_specs=(vmem(), vmem()),
    )(camera_step, point_step)


def solution(mesh):
    in_specs = (
        P(None, None, None, ("sub", "pts")),
        P(None, None, None, ("sub", "pts")),
        P(None, None, ("sub", "pts")),
        P(None, ("sub", "pts")),
        P("sub"),
    )
    out_specs = (P(None, ("sub", "pts")), P(None, ("sub", "pts")))
    return jax.shard_map(
        functools.partial(body, mesh.shape["pts"]),
        mesh=mesh,
        in_specs=in_specs,
        out_specs=out_specs,
        check_vma=False,
    )
```

```python
import functools

import jax
import jax.numpy as jnp
from jax import lax
from jax.experimental import pallas as pl
from jax.experimental.pallas import tpu as pltpu
from jax.sharding import PartitionSpec as P

NCAM = 4096
ITERS = 3
GROUP = 4
NT = (((1,), (1,)), ((), ()))


def cofactor(matrix, row, col):
    kept_rows = [other for other in range(3) if other != row]
    kept_cols = [other for other in range(3) if other != col]
    first = matrix[kept_rows[0]][kept_cols[0]] * matrix[kept_rows[1]][kept_cols[1]]
    second = matrix[kept_rows[0]][kept_cols[1]] * matrix[kept_rows[1]][kept_cols[0]]
    return first - second if (row + col) % 2 == 0 else second - first


def rows_sum(block):
    return jnp.sum(block, axis=0, keepdims=True)


def total_of(block):
    return jnp.sum(rows_sum(block), axis=1, keepdims=True)


def halves_of(block):
    upper = block.astype(jnp.bfloat16).astype(jnp.float32)
    return upper, block - upper


def kernel(
    n,
    cam_far,
    point_far,
    resid_far,
    ids_far,
    damp_ref,
    camera_out,
    point_out,
    cam_ref,
    hot_ref,
    low_ref,
    jac_ref,
    inv_ref,
    pred_ref,
    remain_ref,
    table_ref,
    first_send,
    first_recv,
    part_send,
    part_recv,
    slice_send,
    slice_recv,
    scalar_send,
    scalar_recv,
    cam_given,
    point_ref,
    resid_ref,
    ids_ref,
    load_sems,
    send_sems,
    recv_sems,
):
    me = lax.axis_index("pts")
    views, points = ids_ref.shape
    lanes = camera_out.shape[1]
    params = camera_out.shape[0]
    main = params - 1
    wide = GROUP * lanes
    low = n // GROUP
    damp = damp_ref[0]
    barrier = pltpu.get_barrier_semaphore()
    sent = []

    def greet(step, carry):
        peer = lax.rem(me + 1 + step, n)
        pl.semaphore_signal(
            barrier, inc=1, device_id={"pts": peer}, device_id_type=pl.DeviceIdType.MESH
        )
        return carry

    lax.fori_loop(0, n - 1, greet, 0, unroll=True)
    far = (ids_far, cam_far, point_far, resid_far)
    near = (ids_ref, cam_given, point_ref, resid_ref)
    loads = [
        pltpu.make_async_copy(source, target, load_sems.at[spot])
        for spot, (source, target) in enumerate(zip(far, near))
    ]
    for load in loads:
        load.start()
    loads[0].wait()

    def exchange(phase, source, target):
        def begin(step, carry):
            peer = lax.rem(me + 1 + step, n)
            pltpu.make_async_remote_copy(
                src_ref=source(peer),
                dst_ref=target.at[me],
                send_sem=send_sems.at[phase],
                recv_sem=recv_sems.at[phase],
                device_id={"pts": peer},
                device_id_type=pl.DeviceIdType.MESH,
            ).start()
            return carry

        lax.fori_loop(0, n - 1, begin, 0, unroll=True)
        others = target.at[pl.ds(0, n - 1)]
        sent.append(pltpu.make_async_copy(others, others, send_sems.at[phase]))
        pltpu.make_async_copy(others, others, recv_sems.at[phase]).wait()

    def spread(value):
        return jnp.broadcast_to(value, (1, lanes))

    for view in range(views):
        ids = ids_ref[view : view + 1, :]
        cols = pl.ds(view * points, points)
        lane_ids = lax.bitwise_and(ids, wide - 1) if wide & (wide - 1) == 0 else lax.rem(ids, wide)
        row_ids = (ids - lane_ids) // wide
        high = lax.broadcasted_iota(jnp.int32, (wide, points), 0) == lane_ids
        hot_ref[:, cols] = high.astype(jnp.float32).astype(jnp.bfloat16)
        lows = lax.broadcasted_iota(jnp.int32, (low, points), 0) == row_ids
        low_ref[:, cols] = lows.astype(jnp.float32).astype(jnp.bfloat16)
    for load in loads[1:]:
        load.wait()
    for view in range(views):
        for part in range(2):
            cam_ref[view, part] = cam_given[part, :, view, :]
    for coord in range(3):
        jac_ref[coord] = jnp.concatenate([point_ref[0, coord], point_ref[1, coord]], axis=0)

    gram = [[None] * 3 for unused in range(3)]
    for row in range(3):
        for col in range(row, 3):
            entry = rows_sum(jac_ref[row] * jac_ref[col])
            if row == col:
                entry = entry + damp
            gram[row][col] = entry
            gram[col][row] = entry
    determinant = (
        gram[0][0] * cofactor(gram, 0, 0)
        + gram[0][1] * cofactor(gram, 0, 1)
        + gram[0][2] * cofactor(gram, 0, 2)
    )
    for row in range(3):
        for col in range(3):
            inv_ref[3 * row + col : 3 * row + col + 1, :] = cofactor(gram, col, row) / determinant

    def solve(pulled):
        return [
            sum(inv_ref[3 * row + col : 3 * row + col + 1, :] * pulled[col] for col in range(3))
            for row in range(3)
        ]

    def pull(rows):
        return [rows_sum(jac_ref[coord] * rows) for coord in range(3)]

    def push(solved):
        return sum(jac_ref[coord] * solved[coord] for coord in range(3))

    def at_views(view):
        cols = pl.ds(view * points, points)
        return hot_ref[:, cols], low_ref[:, cols]

    def scatter(values_of):
        totals = None
        for view in range(views):
            hot, lows = at_views(view)
            stacked = []
            for upper_rows, last_row in values_of(view):
                both = jnp.concatenate(halves_of(upper_rows), axis=0).astype(jnp.bfloat16)
                stacked += [both * lows[row : row + 1, :] for row in range(low)]
                stacked += [half.astype(jnp.bfloat16) * lows for half in halves_of(last_row)]
            found = lax.dot_general(
                jnp.concatenate(stacked, axis=0), hot, NT, preferred_element_type=jnp.float32
            )
            totals = found if totals is None else totals + found
        return totals

    def pulled_values(view):
        first = remain_ref[view : view + 1, :]
        second = remain_ref[views + view : views + view + 1, :]
        return (
            cam_ref[view, 0, 0:main, :] * first + cam_ref[view, 1, 0:main, :] * second,
            cam_ref[view, 0, main:params, :] * first + cam_ref[view, 1, main:params, :] * second,
        )

    def squares(view):
        first, second = cam_ref[view, 0], cam_ref[view, 1]
        both = first * first + second * second
        return both[0:main], both[main:params]

    def fill(target, totals, start, offset, last, sign):
        for slot in range(n):
            row, half = slot // GROUP, (slot % GROUP) * lanes
            cols = slice(half, half + lanes)
            first = start + 2 * main * row
            upper = totals[first : first + main, cols] + totals[first + main : first + 2 * main, cols]
            first = start + 2 * main * low + row
            lower = totals[first : first + 1, cols] + totals[first + low : first + low + 1, cols]
            target[slot, offset : offset + main, :] = upper if sign > 0 else -upper
            target[slot, last : last + 1, :] = lower if sign > 0 else -lower

    resid = jnp.concatenate([resid_ref[0], resid_ref[1]], axis=0)
    grad = pull(resid)
    remain_ref[...] = resid - push(solve(grad))
    both_parts = scatter(lambda view: [pulled_values(view), squares(view)])
    fill(first_send, both_parts, 0, 0, 2 * main, -1)
    fill(first_send, both_parts, 2 * low * params, main, 2 * main + 1, 1)
    pl.semaphore_wait(barrier, n - 1)
    first_recv[me] = first_send[me]
    exchange(0, lambda peer: first_send.at[peer], first_recv)
    summed = jnp.sum(first_recv[...], axis=0)
    residual_vec = jnp.concatenate([summed[0:main], summed[2 * main : 2 * main + 1]], axis=0)
    precond = damp + jnp.concatenate(
        [summed[main : 2 * main], summed[2 * main + 1 : 2 * main + 2]], axis=0
    )
    phase = 1
    norm_now = None
    direction = None
    step_sum = None
    pulled_sum = grad
    for iteration in range(ITERS):
        scaled = residual_vec / precond
        slice_send[iteration, 0:params, :] = scaled
        slice_send[iteration, params : params + 1, :] = spread(total_of(residual_vec * scaled))
        mine = slice_recv.at[iteration]
        mine[me] = slice_send[iteration]
        exchange(phase, lambda peer: slice_send.at[iteration], mine)
        phase += 1
        norm_next = jnp.sum(mine[:, params, :], axis=0, keepdims=True)
        factor = None if norm_now is None else norm_next / norm_now
        norm_now = norm_next
        direction = scaled if factor is None else scaled + factor * direction
        for slot in range(n):
            row, half = slot // GROUP, (slot % GROUP) * lanes
            spots = (
                (slice(row * main, (row + 1) * main), slice(0, main)),
                (slice(low * main + row, low * main + row + 1), slice(main, params)),
            )
            for spot, source in spots:
                update = mine[slot, source, :]
                if factor is not None:
                    update = update + factor * table_ref[spot, half : half + lanes]
                table_ref[spot, half : half + lanes] = update
        upper, lower = halves_of(table_ref[...])
        lookup = jnp.concatenate([upper, lower], axis=0).astype(jnp.bfloat16)
        for view in range(views):
            hot, lows = at_views(view)
            lows = lows.astype(jnp.float32)
            picked = jnp.dot(lookup, hot, preferred_element_type=jnp.float32)
            size = low * params
            upper_rows = sum(
                (picked[row * main : (row + 1) * main] + picked[size + row * main : size + (row + 1) * main])
                * lows[row : row + 1]
                for row in range(low)
            )
            last_row = rows_sum((picked[low * main : size] + picked[size + low * main :]) * lows)
            for part in range(2):
                pred_ref[part * views + view : part * views + view + 1, :] = (
                    rows_sum(cam_ref[view, part, 0:main, :] * upper_rows)
                    + cam_ref[view, part, main:params, :] * last_row
                )
        predicted = pred_ref[...]
        pulled = pull(predicted)
        remain = predicted - push(solve(pulled))
        curve_part = spread(total_of(predicted * remain) + damp * total_of(direction * direction))
        if iteration + 1 < ITERS:
            remain_ref[...] = remain
            image_part = scatter(lambda view: [pulled_values(view)])
            outgoing = part_send.at[iteration]
            incoming = part_recv.at[iteration]
            fill(outgoing, image_part, 0, 0, main, 1)
            for slot in range(n):
                outgoing[slot, params : params + 1, :] = curve_part
            incoming[me] = outgoing[me]
            exchange(phase, lambda peer: outgoing.at[peer], incoming)
            phase += 1
            summed = jnp.sum(incoming[...], axis=0)
            image = damp * direction + summed[0:params]
            curve = summed[params : params + 1]
        else:
            scalar_send[...] = curve_part
            scalar_recv[me] = curve_part
            exchange(phase, lambda peer: scalar_send, scalar_recv)
            curve = jnp.sum(scalar_recv[...], axis=0)
        step_size = norm_now / curve
        moved = step_size * direction
        step_sum = moved if step_sum is None else step_sum + moved
        wide_step = jnp.concatenate([step_size] * (points // lanes), axis=1)
        pulled_sum = [old + wide_step * new for old, new in zip(pulled_sum, pulled)]
        if iteration + 1 < ITERS:
            residual_vec = residual_vec - step_size * image
    camera_out[...] = step_sum
    for copy in sent:
        copy.wait()
    solved = solve(pulled_sum)
    for coord in range(3):
        point_out[coord : coord + 1, :] = solved[coord]


def hand_on(camera_ref, point_ref, camera_out, point_out):
    camera_out[...] = camera_ref[...]
    point_out[...] = -point_ref[...]


def body(n, cam_jac, point_jac, residuals, obs_camera, damping):
    params = cam_jac.shape[1]
    views, points = obs_camera.shape
    lanes = NCAM // n
    wide, low = GROUP * lanes, n // GROUP
    main = params - 1
    phases = 2 * ITERS + 1
    vmem = functools.partial(pl.BlockSpec, memory_space=pltpu.VMEM)
    camera_step, point_step = pl.pallas_call(
        functools.partial(kernel, n),
        name="schur_solve",
        out_shape=(
            jax.ShapeDtypeStruct((params, lanes), jnp.float32),
            jax.ShapeDtypeStruct((3, points), jnp.float32),
        ),
        in_specs=[pl.BlockSpec(memory_space=pl.ANY)] * 4 + [pl.BlockSpec(memory_space=pltpu.SMEM)],
        out_specs=(vmem(), vmem()),
        scratch_shapes=[
            pltpu.VMEM((views, 2, params, points), jnp.float32),
            pltpu.VMEM((wide, views * points), jnp.bfloat16),
            pltpu.VMEM((low, views * points), jnp.bfloat16),
            pltpu.VMEM((3, 2 * views, points), jnp.float32),
            pltpu.VMEM((9, points), jnp.float32),
            pltpu.VMEM((2 * views, points), jnp.float32),
            pltpu.VMEM((2 * views, points), jnp.float32),
            pltpu.VMEM((low * params, wide), jnp.float32),
            pltpu.VMEM((n, 2 * params, lanes), jnp.float32),
            pltpu.VMEM((n, 2 * params, lanes), jnp.float32),
            pltpu.VMEM((ITERS - 1, n, params + 1, lanes), jnp.float32),
            pltpu.VMEM((ITERS - 1, n, params + 1, lanes), jnp.float32),
            pltpu.VMEM((ITERS, params + 1, lanes), jnp.float32),
            pltpu.VMEM((ITERS, n, params + 1, lanes), jnp.float32),
            pltpu.VMEM((1, lanes), jnp.float32),
            pltpu.VMEM((n, 1, lanes), jnp.float32),
            pltpu.VMEM(cam_jac.shape, jnp.float32),
            pltpu.VMEM(point_jac.shape, jnp.float32),
            pltpu.VMEM(residuals.shape, jnp.float32),
            pltpu.VMEM(obs_camera.shape, jnp.int32),
            pltpu.SemaphoreType.DMA((4,)),
            pltpu.SemaphoreType.DMA((phases,)),
            pltpu.SemaphoreType.DMA((phases,)),
        ],
        compiler_params=pltpu.CompilerParams(collective_id=0, has_side_effects=True),
    )(
        cam_jac,
        point_jac,
        residuals,
        obs_camera,
        damping,
    )
    return pl.pallas_call(
        hand_on,
        name="hand_on",
        out_shape=(
            jax.ShapeDtypeStruct(camera_step.shape, jnp.float32),
            jax.ShapeDtypeStruct(point_step.shape, jnp.float32),
        ),
        in_specs=[vmem(), vmem()],
        out_specs=(vmem(), vmem()),
    )(camera_step, point_step)


def solution(mesh):
    in_specs = (
        P(None, None, None, ("sub", "pts")),
        P(None, None, None, ("sub", "pts")),
        P(None, None, ("sub", "pts")),
        P(None, ("sub", "pts")),
        P("sub"),
    )
    out_specs = (P(None, ("sub", "pts")), P(None, ("sub", "pts")))
    return jax.shard_map(
        functools.partial(body, mesh.shape["pts"]),
        mesh=mesh,
        in_specs=in_specs,
        out_specs=out_specs,
        check_vma=False,
    )
```
